1024 devices in a mesh: ctx: 32 (over x, z_hi, core), tp: 32 (over y, z_lo).
Axes of the slice: x: 4, y: 4, z: 32 (z_hi: 4, z_lo: 8; z = z_hi * 8 + z_lo), core: 2. Of those that a mesh axis runs over, the one named last changes fastest.
Arguments:
- query_feats: bfloat16 [8192, 4096], P('tp', 'ctx'), may hold values from -6 to 6
- key_feats: bfloat16 [8192, 4096], P('tp', 'ctx'), may hold values from -6 to 6
- value_feats: bfloat16 [8192, 4096], P('tp', 'ctx'), may hold values from -6 to 6
- out_gate: bfloat16 [8192, 4096], P('tp', 'ctx'), may hold values from -6 to 6
- mr_filter: bfloat16 [512, 128], P('tp'), may hold values from -0.5 to 0.5
- lr_rates: float32 [512, 16], P('tp'), may hold values from 0.00012207031 to 0.1
- lr_residues: float32 [512, 16], P('tp'), may hold values from -6 to 6
- w_out: bfloat16 [8192, 8192], P('tp'), may hold values from -0.125 to 0.125
Outputs:
- mixed_out: bfloat16 [8192, 4096], P('tp', 'ctx')
The draws below stay inside these ranges and needn't reach their ends.
All inputs are finite; a program needn't handle non-finite values.
Results may differ from the reference program's by a relative error of at most 0.023.
Values may be sent and summed in bfloat16 or wider, within the bound.
No kernel may reach another device: no remote copies, remote signals or barrier semaphores. Data moves between devices by JAX's collectives and lax.ppermute only.
A program may use at most 32 MiB of HBM per device.

```python
import math
import jax
import jax.numpy as jnp
from jax import lax

D = 8192
MR_TAPS = 128
ORDER = 16
SEQ = 4096
N_TP = 32


def strengthened(values, key, source, target, shards_of, factor):
    def block_of(position):
        return (jnp.arange(values.shape[position]) // (values.shape[position] // shards_of)).reshape((-1,) + (1,) * (values.ndim - 1 - position))

    near = jax.random.permutation(key, shards_of)[block_of(target)]
    far = (block_of(target) + shards_of // 2) % shards_of
    return jnp.where((block_of(source) == near) | (block_of(source) == far), factor * values, values)


def block_scale(key, dims, split, least, largest):
    gain = 1.0
    for position, parts in split:
        draws = jax.random.uniform(jax.random.fold_in(jax.random.fold_in(key, 6), position), (parts,), jnp.float32, least / len(split), largest / len(split))
        gain = gain * jnp.repeat(jnp.exp(draws), dims[position] // parts).reshape((-1,) + (1,) * (len(dims) - 1 - position))
    return gain


def noise(key, extent, width, bound, split=(), kind=jnp.bfloat16):
    array = width * jax.random.normal(key, extent, jnp.float32)
    if split:
        array = array * block_scale(key, extent, split, -0.22, 0.18)
    return jnp.clip(array, -bound, bound).astype(kind)


def noise_with(stream_key, shape, width, bound, cuts, heavy, dtype=jnp.bfloat16):
    drawn = width * jax.random.normal(stream_key, shape, jnp.float32)
    if cuts:
        drawn = drawn * block_scale(stream_key, shape, cuts, -0.22, 0.18)
    return jnp.clip(strengthened(drawn, jax.random.fold_in(stream_key, 3), *heavy), -bound, bound).astype(dtype)


def setup_inputs(seed: int = 0) -> dict:
    key_of = jax.random.split(jax.random.key(seed), 9)
    return {
        "query_feats": noise(key_of[0], (D, SEQ), 1.0, 6.0, ((0, 32), (1, 32))),
        "key_feats": noise(key_of[1], (D, SEQ), 1.0, 6.0, ((0, 32), (1, 32))),
        "value_feats": noise(key_of[2], (D, SEQ), 1.0, 6.0, ((0, 32), (1, 32))),
        "out_gate": noise(key_of[3], (D, SEQ), 1.0, 6.0, ((0, 32), (1, 32))),
        "mr_filter": noise(key_of[4], (D // 16, MR_TAPS), MR_TAPS ** -0.5, 0.5, ((0, 32),)),
        "lr_rates": jnp.clip(jnp.exp(math.log(0.1) - 6.7083283 * jax.random.uniform(key_of[5], (D // 16, ORDER), jnp.float32) ** block_scale(key_of[5], (D // 16, ORDER), ((0, 32),), -0.2, 0.2)), 0.00012207031, 0.1),
        "lr_residues": noise(key_of[6], (D // 16, ORDER), 1.0, 6.0, ((0, 32),), jnp.float32),
        "w_out": noise_with(key_of[7], (D, D), D ** -0.5, 0.125, ((0, 32),), (0, 1, 32, 2.75)),
    }


def lr_filter(decay_rates, residues_in, length):
    positions = jnp.arange(length).astype(jnp.float32)
    decays = jnp.exp(-decay_rates[:, :, None] * positions[None, None, :])
    weights = residues_in * jnp.sqrt(2.0 * decay_rates / decay_rates.shape[1])
    return lax.optimization_barrier(jnp.sum(weights[:, :, None] * decays, axis=1))

def causal_conv(signal, filter_taps):
    length = signal.shape[1]
    fft_size = 2 * length
    group_count = filter_taps.shape[0]
    grouped = signal.astype(jnp.float32).reshape(group_count, -1, length)

    def convolve(pair_in):
        signal_part, taps_part = pair_in
        spectrum = jnp.fft.rfft(signal_part, n=fft_size, axis=-1)
        response = jnp.fft.rfft(taps_part, n=fft_size)
        return jnp.fft.irfft(spectrum * response[None, :], n=fft_size, axis=-1)[:, :length]
    result = lax.map(convolve, (grouped, filter_taps.astype(jnp.float32)))
    return result.reshape(signal.shape)

def reference(query_feats, key_feats, value_feats, out_gate, mr_filter, lr_rates, lr_residues, w_out):
    kv_prod = (key_feats.astype(jnp.float32) * value_feats.astype(jnp.float32)).astype(jnp.bfloat16)
    medium = causal_conv(kv_prod, mr_filter)
    gated_mid = (query_feats.astype(jnp.float32) * medium).astype(jnp.bfloat16)
    long_taps = lr_filter(lr_rates, lr_residues, SEQ)
    long_out = causal_conv(gated_mid, long_taps).astype(jnp.bfloat16)
    gated_out = (out_gate.astype(jnp.float32) * long_out.astype(jnp.float32)).astype(jnp.bfloat16)
    block_rows = D // N_TP
    gate_blocks = gated_out.reshape(N_TP, block_rows, SEQ)
    weight_blocks = w_out.reshape(N_TP, block_rows, D)

    def add_block(running, pair_in):
        gate_part, weight_part = pair_in
        partial_sum = lax.dot_general(weight_part.astype(jnp.float32), gate_part.astype(jnp.float32), (((0,), (0,)), ((), ())))
        rounded = lax.optimization_barrier(partial_sum.astype(jnp.bfloat16))
        return (running + rounded.astype(jnp.float32), None)
    running, unused = lax.scan(add_block, jnp.zeros((D, SEQ), jnp.float32), (gate_blocks, weight_blocks))
    return running.astype(jnp.bfloat16)
```

```python
import jax
import jax.numpy as jnp
from jax import lax
from jax.experimental import pallas as pl
from jax.experimental.pallas import tpu as pltpu
from jax.sharding import Mesh
from jax.sharding import PartitionSpec as P

chan_group = 16
tp_axes = ("y", "zq", "zb")
f32 = jnp.float32
bf16 = jnp.bfloat16


def split_hi_lo(value):
    hi = value.astype(bf16)
    lo = (value - hi.astype(f32)).astype(bf16)
    return hi, lo


def dot(lhs, rhs):
    return lax.dot_general(lhs, rhs, (((1,), (0,)), ((), ())), preferred_element_type=f32)


def shifted(value, rows):
    pad = jnp.zeros((rows, value.shape[1]), value.dtype)
    return jnp.concatenate([pad, value[: value.shape[0] - rows]], axis=0)


def picked_row(table, row):
    rows = lax.broadcasted_iota(jnp.int32, table.shape, 0)
    return jnp.sum(jnp.where(rows == row, table, 0.0), axis=0, keepdims=True)


def circulant(row, size):
    return pltpu.roll(jnp.broadcast_to(row, (size, size)), 0, 1, stride=1, stride_axis=0)


def filters_kernel(group_ref, feats_ref, taps_ref, rates_ref, residues_ref, out_ref):
    block_count, pair_rows, block = feats_ref.shape
    chans = pair_rows // 2
    rows = block_count * chans
    group = group_ref[0]
    mr_taps = picked_row(taps_ref[...].astype(f32), group)
    rates = picked_row(rates_ref[...], group)
    residues = picked_row(residues_ref[...], group)
    modes = rates.shape[1]

    source = lax.broadcasted_iota(jnp.int32, (block, block), 0)
    target = lax.broadcasted_iota(jnp.int32, (block, block), 1)
    causal = target >= source
    mr_circ = circulant(mr_taps, block)
    mr_toeplitz = jnp.concatenate(
        [jnp.where(causal, mr_circ, 0.0), jnp.where(causal, 0.0, mr_circ)], axis=0
    ).astype(bf16)

    steps = lax.broadcasted_iota(jnp.int32, (block, modes), 0).astype(f32)
    weights = residues * jnp.sqrt(2.0 * rates / modes)
    spread = weights * jnp.exp(-rates * steps)
    collect = jnp.exp(-rates * (block - steps))
    lr_taps = lax.dot_general(
        jnp.ones((8, modes), f32),
        spread,
        (((1,), (1,)), ((), ())),
        precision=lax.Precision.HIGHEST,
        preferred_element_type=f32,
    )[:1]
    lr_hi, lr_lo = split_hi_lo(jnp.where(causal, circulant(lr_taps, block), 0.0))
    collect_hi, collect_lo = split_hi_lo(collect)

    feats = feats_ref[...].astype(f32)
    query = feats[:, :chans].reshape(rows, block)
    kv_prod = feats[:, chans:].reshape(rows, block)
    both = jnp.concatenate([kv_prod, shifted(kv_prod, chans)], axis=1).astype(bf16)
    gated = (query * dot(both, mr_toeplitz)).astype(bf16)

    state = dot(gated, collect_hi) + dot(gated, collect_lo)
    state = shifted(state, chans)
    span = 1
    while span < block_count:
        state = state + jnp.exp(-rates * (block * span)) * shifted(state, chans * span)
        span *= 2
    carried = lax.dot_general(
        state,
        spread,
        (((1,), (1,)), ((), ())),
        precision=lax.Precision.HIGHEST,
        preferred_element_type=f32,
    )
    long_out = dot(gated, lr_hi) + dot(gated, lr_lo) + carried
    out_ref[...] = long_out.reshape(block_count, chans, block).astype(bf16)


def filtered(group, feats, mr_filter, lr_rates, lr_residues):
    block_count, pair_rows, block = feats.shape
    vmem = pl.BlockSpec(memory_space=pltpu.VMEM)
    return pl.pallas_call(
        filters_kernel,
        out_shape=jax.ShapeDtypeStruct((block_count, pair_rows // 2, block), bf16),
        in_specs=[pl.BlockSpec(memory_space=pltpu.SMEM), vmem, vmem, vmem, vmem],
        out_specs=vmem,
    )(group, feats, mr_filter, lr_rates, lr_residues)


def project_kernel(gate_ref, long_ref, w_ref, out_ref, held_ref):
    _, low_count, mid_count, tokens, width = out_ref.shape

    @pl.when(pl.program_id(0) == 0)
    def _():
        product = gate_ref[...].astype(f32) * long_ref[...].astype(f32)
        held_ref[...] = product.T.astype(bf16)

    held = held_ref[...]
    for mid in range(mid_count):
        for low in range(low_count):
            first = (mid * low_count + low) * width
            out_ref[0, low, mid] = dot(held, w_ref[:, first : first + width]).astype(bf16)


def projected(out_gate, long_out, w_out, y_count, mid_count, low_count):
    channels, tokens = out_gate.shape
    width = w_out.shape[1] // (y_count * mid_count * low_count)
    small = pl.BlockSpec((channels, tokens), lambda i: (0, 0))
    return pl.pallas_call(
        project_kernel,
        grid=(y_count,),
        out_shape=jax.ShapeDtypeStruct((y_count, low_count, mid_count, tokens, width), bf16),
        in_specs=[
            small,
            small,
            pl.BlockSpec((channels, mid_count * low_count * width), lambda i: (0, i)),
        ],
        out_specs=pl.BlockSpec(
            (1, low_count, mid_count, tokens, width), lambda i: (i, 0, 0, 0, 0)
        ),
        scratch_shapes=[pltpu.VMEM((tokens, channels), bf16)],
    )(out_gate, long_out, w_out)


def per_device(
    query_feats, key_feats, value_feats, out_gate, mr_filter, lr_rates, lr_residues, w_out
):
    channels, tokens = key_feats.shape
    ctx_count = lax.axis_size("ctx")
    piece = channels // ctx_count
    kv_prod = (key_feats.astype(f32) * value_feats.astype(f32)).astype(bf16)
    pair = jnp.concatenate(
        [query_feats.reshape(ctx_count, piece, tokens), kv_prod.reshape(ctx_count, piece, tokens)],
        axis=1,
    )
    feats = lax.all_to_all(pair, "ctx", split_axis=0, concat_axis=0, tiled=True)
    group = (lax.axis_index("ctx") * piece // chan_group).astype(jnp.int32).reshape(1)
    long_out = filtered(group, feats, mr_filter, lr_rates, lr_residues)
    returned = lax.all_to_all(long_out, "ctx", split_axis=0, concat_axis=0, tiled=True)
    y_count, mid_count, low_count = (lax.axis_size(name) for name in tp_axes)
    partial = projected(
        out_gate, returned.reshape(channels, tokens), w_out, y_count, mid_count, low_count
    )
    width = partial.shape[-1]
    near = lax.all_to_all(
        partial.reshape(y_count * low_count, mid_count, tokens, width),
        ("y", "zb"),
        split_axis=0,
        concat_axis=0,
        tiled=True,
    )
    near_sum = jnp.sum(near.astype(f32), axis=0).astype(bf16)
    far = lax.all_to_all(near_sum, "zq", split_axis=0, concat_axis=0, tiled=True)
    return jnp.sum(far.astype(f32), axis=0).T.astype(bf16)


def solution(mesh):
    ctx_count, tp_count = mesh.devices.shape
    finer = Mesh(
        mesh.devices.reshape(ctx_count, tp_count // 8, 4, 2), ("ctx",) + tp_axes
    )
    tiled = P(tp_axes, "ctx")
    rows = P(tp_axes, None)
    return jax.shard_map(
        per_device,
        mesh=finer,
        in_specs=(tiled, tiled, tiled, tiled, rows, rows, rows, rows),
        out_specs=tiled,
        check_vma=False,
    )
```

```python
import jax
import jax.numpy as jnp
from jax import lax
from jax.experimental import pallas as pl
from jax.experimental.pallas import tpu as pltpu
from jax.sharding import Mesh
from jax.sharding import PartitionSpec as P

chan_group = 16
ctx_axes = ("x", "zh", "co")
tp_axes = ("y", "zq", "zb")
f32 = jnp.float32
bf16 = jnp.bfloat16


def split_hi_lo(value):
    hi = value.astype(bf16)
    lo = (value - hi.astype(f32)).astype(bf16)
    return hi, lo


def dot(lhs, rhs, left=1, right=0, precision=None):
    return lax.dot_general(
        lhs,
        rhs,
        (((left,), (right,)), ((), ())),
        precision=precision,
        preferred_element_type=f32,
    )


def circulant(row, size):
    return pltpu.roll(jnp.broadcast_to(row, (size, size)), 0, 1, stride=1, stride_axis=0)


def same_group(row_count, col_count, row_width):
    rows = lax.broadcasted_iota(jnp.int32, (row_count, col_count), 0) // row_width
    cols = lax.broadcasted_iota(jnp.int32, (row_count, col_count), 1) // chan_group
    return rows == cols


def tables_kernel(taps_ref, rates_ref, residues_ref, mr_ref, lr_ref, collect_ref, spread_ref):
    group_count, block = taps_ref.shape
    mode_rows = rates_ref.shape[0]
    modes = mode_rows // group_count
    source = lax.broadcasted_iota(jnp.int32, (block, block), 0)
    target = lax.broadcasted_iota(jnp.int32, (block, block), 1)
    causal = target >= source

    rates = rates_ref[...]
    steps = lax.broadcasted_iota(jnp.int32, (mode_rows, block), 1).astype(f32)
    spread = residues_ref[...] * jnp.sqrt(2.0 * rates / modes) * jnp.exp(-rates * steps)
    spread_ref[...] = spread
    collect_hi, collect_lo = split_hi_lo(jnp.exp(-rates * (block - steps)))
    collect_ref[0] = collect_hi
    collect_ref[1] = collect_lo
    lr_taps = jnp.sum(spread.reshape(group_count, modes, block), axis=1)
    mr_taps = taps_ref[...].astype(f32)
    for group in range(group_count):
        mr_circ = circulant(mr_taps[group : group + 1], block)
        mr_ref[group, :block] = jnp.where(causal, mr_circ, 0.0).astype(bf16)
        mr_ref[group, block:] = jnp.where(causal, 0.0, mr_circ).astype(bf16)
        lr_circ = jnp.where(causal, circulant(lr_taps[group : group + 1], block), 0.0)
        lr_hi, lr_lo = split_hi_lo(lr_circ)
        lr_ref[group, :, :block] = lr_hi
        lr_ref[group, :, block:] = lr_lo


def blocks_kernel(query_ref, kv_ref, rim_ref, mr_ref, lr_ref, collect_ref, state_ref, local_ref):
    channels, block = kv_ref.shape
    group_count = mr_ref.shape[0]
    modes = state_ref.shape[0]
    both = jnp.concatenate([kv_ref[...], rim_ref[...]], axis=1)
    query = query_ref[...].astype(f32)
    gated_parts = []
    for group in range(group_count):
        rows = slice(group * chan_group, (group + 1) * chan_group)
        medium = dot(both[rows], mr_ref[group])
        gated = (query[rows] * medium).astype(bf16)
        wide = dot(gated, lr_ref[group])
        local_ref[rows] = wide[:, :block] + wide[:, block:]
        gated_parts.append(gated)
    gated = jnp.concatenate(gated_parts, axis=0)
    mixed = dot(collect_ref[0], gated, 1, 1) + dot(collect_ref[1], gated, 1, 1)
    mixed = jnp.where(same_group(group_count * modes, channels, modes), mixed, 0.0)
    state_ref[...] = jnp.sum(mixed.reshape(group_count, modes, channels), axis=0)


def rows_kernel(place_ref, near_ref, rates_ref, out_ref, *, block):
    z_count = out_ref.shape[0]
    near_count = near_ref.shape[0]
    x_here, z_here, core_here = place_ref[0], place_ref[1], place_ref[2]
    span = -block * rates_ref[...]
    for z_to in range(z_count):
        total = jnp.zeros(out_ref.shape[1:], f32)
        target = (x_here * z_count + z_to) * 2 + core_here
        for near in range(near_count):
            source = (near // 2 * z_count + z_here) * 2 + near % 2
            gap = target - 1 - source
            decay = jnp.exp(span * jnp.maximum(gap, 0).astype(f32))
            total = total + jnp.where(gap >= 0, decay, 0.0) * near_ref[near]
        out_ref[z_to] = total


def project_kernel(gate_ref, local_ref, far_ref, spread_ref, w_ref, out_ref, held_ref):
    _, low_count, mid_count, tokens, width = out_ref.shape
    far_count, modes, channels = far_ref.shape

    @pl.when(pl.program_id(0) == 0)
    def _():
        state = far_ref[0]
        for far in range(1, far_count):
            state = state + far_ref[far]
        mode_rows = spread_ref.shape[0]
        wide = jnp.concatenate([state] * (mode_rows // modes), axis=0)
        wide = jnp.where(same_group(mode_rows, channels, modes), wide, 0.0)
        carried = dot(wide, spread_ref[...], 0, 0, lax.Precision.HIGHEST)
        long_out = (local_ref[...] + carried).astype(bf16)
        product = gate_ref[...].astype(f32) * long_out.astype(f32)
        held_ref[...] = product.T.astype(bf16)

    held = held_ref[...]
    for mid in range(mid_count):
        for low in range(low_count):
            first = (mid * low_count + low) * width
            out_ref[0, low, mid] = dot(held, w_ref[:, first : first + width]).astype(bf16)


def per_device(
    query_feats, key_feats, value_feats, out_gate, mr_filter, lr_rates, lr_residues, w_out
):
    channels, tokens = key_feats.shape
    group_count, modes = lr_rates.shape
    ctx_count = lax.axis_size(ctx_axes)
    z_count = lax.axis_size("zh")
    vmem = pl.BlockSpec(memory_space=pltpu.VMEM)
    smem = pl.BlockSpec(memory_space=pltpu.SMEM)

    kv_prod = (key_feats.astype(f32) * value_feats.astype(f32)).astype(bf16)
    rim = lax.ppermute(kv_prod, ctx_axes, [(i, i + 1) for i in range(ctx_count - 1)])
    mode_rows = group_count * modes
    mr_table, lr_table, collect, spread = pl.pallas_call(
        tables_kernel,
        out_shape=(
            jax.ShapeDtypeStruct((group_count, 2 * tokens, tokens), bf16),
            jax.ShapeDtypeStruct((group_count, tokens, 2 * tokens), bf16),
            jax.ShapeDtypeStruct((2, mode_rows, tokens), bf16),
            jax.ShapeDtypeStruct((mode_rows, tokens), f32),
        ),
        in_specs=[vmem] * 3,
        out_specs=(vmem,) * 4,
    )(mr_filter, lr_rates.reshape(mode_rows, 1), lr_residues.reshape(mode_rows, 1))
    rates_wide = jnp.repeat(lr_rates.T, chan_group, axis=1)
    state, local = pl.pallas_call(
        blocks_kernel,
        out_shape=(
            jax.ShapeDtypeStruct((modes, channels), f32),
            jax.ShapeDtypeStruct((channels, tokens), f32),
        ),
        in_specs=[vmem] * 6,
        out_specs=(vmem,) * 2,
    )(query_feats, kv_prod, rim, mr_table, lr_table, collect)
    near_count = lax.axis_size(("x", "co"))
    near_states = lax.all_to_all(
        jnp.broadcast_to(state[None], (near_count, modes, channels)),
        ("x", "co"),
        split_axis=0,
        concat_axis=0,
        tiled=True,
    )
    place = jnp.stack([lax.axis_index(name) for name in ctx_axes]).astype(jnp.int32)
    row_states = pl.pallas_call(
        lambda *refs: rows_kernel(*refs, block=tokens),
        out_shape=jax.ShapeDtypeStruct((z_count, modes, channels), f32),
        in_specs=[smem, vmem, vmem],
        out_specs=vmem,
        name="rows_kernel",
    )(place, near_states, rates_wide)
    far_states = lax.all_to_all(row_states, "zh", split_axis=0, concat_axis=0, tiled=True)

    y_count, mid_count, low_count = (lax.axis_size(name) for name in tp_axes)
    width = w_out.shape[1] // (y_count * mid_count * low_count)
    small = lambda *shape: pl.BlockSpec(shape, lambda i: (0,) * len(shape))
    partial = pl.pallas_call(
        project_kernel,
        grid=(y_count,),
        out_shape=jax.ShapeDtypeStruct((y_count, low_count, mid_count, tokens, width), bf16),
        in_specs=[
            small(channels, tokens),
            small(channels, tokens),
            small(z_count, modes, channels),
            small(mode_rows, tokens),
            pl.BlockSpec((channels, mid_count * low_count * width), lambda i: (0, i)),
        ],
        out_specs=pl.BlockSpec(
            (1, low_count, mid_count, tokens, width), lambda i: (i, 0, 0, 0, 0)
        ),
        scratch_shapes=[pltpu.VMEM((tokens, channels), bf16)],
    )(out_gate, local, far_states, spread, w_out)
    near = lax.all_to_all(
        partial.reshape(y_count * low_count, mid_count, tokens, width),
        ("y", "zb"),
        split_axis=0,
        concat_axis=0,
        tiled=True,
    )
    near_sum = jnp.sum(near.astype(f32), axis=0).astype(bf16)
    far = lax.all_to_all(near_sum, "zq", split_axis=0, concat_axis=0, tiled=True)
    return jnp.sum(far.astype(f32), axis=0).T.astype(bf16)


def solution(mesh):
    ctx_count, tp_count = mesh.devices.shape
    finer = Mesh(
        mesh.devices.reshape(ctx_count // 8, 4, 2, tp_count // 8, 4, 2), ctx_axes + tp_axes
    )
    tiled = P(tp_axes, ctx_axes)
    rows = P(tp_axes, None)
    return jax.shard_map(
        per_device,
        mesh=finer,
        in_specs=(tiled, tiled, tiled, tiled, rows, rows, rows, rows),
        out_specs=tiled,
        check_vma=False,
    )
```

```python
import jax
import jax.numpy as jnp
from jax import lax
from jax.experimental import pallas as pl
from jax.experimental.pallas import tpu as pltpu
from jax.sharding import Mesh
from jax.sharding import PartitionSpec as P


chan_group = 16
ctx_axes = ("x", "zh", "co")
tp_axes = ("y", "zq", "zb")
f32 = jnp.float32
bf16 = jnp.bfloat16


def split_hi_lo(value):
    hi = value.astype(bf16)
    lo = (value - hi.astype(f32)).astype(bf16)
    return hi, lo


def dot(lhs, rhs, left=1, right=0, precision=None):
    return lax.dot_general(
        lhs,
        rhs,
        (((left,), (right,)), ((), ())),
        precision=precision,
        preferred_element_type=f32,
    )


def circulant(row, size):
    return pltpu.roll(jnp.broadcast_to(row, (size, size)), 0, 1, stride=1, stride_axis=0)


def same_block(row_count, col_count, row_width, col_width):
    rows = lax.broadcasted_iota(jnp.int32, (row_count, col_count), 0) // row_width
    cols = lax.broadcasted_iota(jnp.int32, (row_count, col_count), 1) // col_width
    return rows == cols


def laid_out(table):
    rows, cols = table.shape
    tiled = jnp.concatenate([table] * rows, axis=1)
    kept = jnp.where(same_block(rows, rows * cols, 1, cols), tiled, 0.0)
    return jnp.sum(kept, axis=0, keepdims=True)


def tables_kernel(
    place_ref,
    taps_ref,
    rates_ref,
    residues_ref,
    gate_ref,
    query_ref,
    mr_ref,
    lr_ref,
    collect_ref,
    spread_ref,
    decay_ref,
    held_gate_ref,
    held_query_ref,
):
    held_gate_ref[...] = gate_ref[...].astype(f32).T
    held_query_ref[...] = query_ref[...].astype(f32)
    group_count, block = taps_ref.shape
    modes = rates_ref.shape[1]
    mode_cols = group_count * modes
    z_count, near_count, _, channels = decay_ref.shape
    source = lax.broadcasted_iota(jnp.int32, (block, block), 0)
    target = lax.broadcasted_iota(jnp.int32, (block, block), 1)
    causal = target >= source

    rates = laid_out(rates_ref[...])
    weights = laid_out(residues_ref[...]) * jnp.sqrt(2.0 * rates / modes)
    steps = lax.broadcasted_iota(jnp.int32, (block, mode_cols), 0).astype(f32)
    spread = weights * jnp.exp(-rates * steps)
    spread_ref[0], spread_ref[1] = split_hi_lo(spread)
    collect = jnp.exp(-rates * (block - steps)).T
    collect_ref[0], collect_ref[1] = split_hi_lo(collect)
    pick = same_block(group_count, mode_cols, 1, modes).astype(f32)
    lr_taps = dot(pick, spread, 1, 1, lax.Precision.HIGHEST)
    mr_taps = taps_ref[...].astype(f32)
    for group in range(group_count):
        mr_circ = circulant(mr_taps[group : group + 1], block)
        mr_ref[group, :block] = jnp.where(causal, mr_circ, 0.0).astype(bf16)
        mr_ref[group, block:] = jnp.where(causal, 0.0, mr_circ).astype(bf16)
        lr_circ = jnp.where(causal, circulant(lr_taps[group : group + 1], block), 0.0)
        lr_hi, lr_lo = split_hi_lo(lr_circ)
        lr_ref[group, :, :block] = lr_hi
        lr_ref[group, :, block:] = lr_lo

    owner = same_block(group_count, channels, 1, chan_group).astype(f32)
    span = -block * dot(rates_ref[...], owner, 0, 0, lax.Precision.HIGHEST)
    x_here, z_here, core_here = place_ref[0], place_ref[1], place_ref[2]
    for z_to in range(z_count):
        into = (x_here * z_count + z_to) * 2 + core_here
        for near in range(near_count):
            out_of = (near // 2 * z_count + z_here) * 2 + near % 2
            gap = into - 1 - out_of
            decay = jnp.exp(span * jnp.maximum(gap, 0).astype(f32))
            decay_ref[z_to, near] = jnp.where(gap >= 0, decay, 0.0)


def blocks_kernel(query_ref, kv_ref, rim_ref, mr_ref, collect_ref, state_ref, gated_ref):
    channels, _ = kv_ref.shape
    group_count = mr_ref.shape[0]
    near_count, modes, _ = state_ref.shape
    both = jnp.concatenate([kv_ref[...], rim_ref[...]], axis=1)
    query = query_ref[...]
    gated_parts = []
    for group in range(group_count):
        rows = slice(group * chan_group, (group + 1) * chan_group)
        medium = dot(both[rows], mr_ref[group])
        gated_parts.append((query[rows] * medium).astype(bf16))
    gated = jnp.concatenate(gated_parts, axis=0)
    gated_ref[...] = gated
    mixed = dot(collect_ref[0], gated, 1, 1) + dot(collect_ref[1], gated, 1, 1)
    mixed = jnp.where(same_block(group_count * modes, channels, modes, chan_group), mixed, 0.0)
    state = jnp.sum(mixed.reshape(group_count, modes, channels), axis=0)
    for near in range(near_count):
        state_ref[near] = state


def local_kernel(gated_ref, lr_ref, local_ref):
    group_count, block, _ = lr_ref.shape
    parts = []
    for group in range(group_count):
        rows = slice(group * chan_group, (group + 1) * chan_group)
        wide = dot(gated_ref[rows], lr_ref[group])
        parts.append(wide[:, :block] + wide[:, block:])
    local_ref[...] = jnp.concatenate(parts, axis=0).T


def rows_kernel(near_ref, decay_ref, out_ref):
    for z_to in range(out_ref.shape[0]):
        total = decay_ref[z_to, 0] * near_ref[0]
        for near in range(1, near_ref.shape[0]):
            total = total + decay_ref[z_to, near] * near_ref[near]
        out_ref[z_to] = total


def project_kernel(gate_ref, local_ref, far_ref, spread_ref, w_hbm, out_ref, w_ref, sems):
    y_count, low_count, mid_count, _, width = out_ref.shape
    span = low_count * mid_count * width
    copies = []
    for y_to in range(y_count):
        cols = slice(y_to * span, (y_to + 1) * span)
        copies.append(
            pltpu.make_async_copy(w_hbm.at[:, cols], w_ref.at[:, cols], sems.at[y_to])
        )
        copies[-1].start()
    far_count, modes, channels = far_ref.shape
    state = far_ref[0]
    for far in range(1, far_count):
        state = state + far_ref[far]
    mode_rows = spread_ref.shape[2]
    wide = jnp.concatenate([state] * (mode_rows // modes), axis=0)
    wide = jnp.where(same_block(mode_rows, channels, modes, chan_group), wide, 0.0)
    wide_hi, wide_lo = split_hi_lo(wide)
    carried = dot(spread_ref[0], wide_hi) + dot(spread_ref[0], wide_lo)
    carried = carried + dot(spread_ref[1], wide_hi)
    long_out = (local_ref[...] + carried).astype(bf16)
    held = (gate_ref[...] * long_out.astype(f32)).astype(bf16)
    for y_to in range(y_count):
        copies[y_to].wait()
        for mid in range(mid_count):
            for low in range(low_count):
                first = ((y_to * mid_count + mid) * low_count + low) * width
                total = dot(held, w_ref[:, first : first + width])
                out_ref[y_to, low, mid] = total.astype(bf16)


def on_chip(kernel, outs, *args, raw=(), scratch=()):
    vmem = pl.BlockSpec(memory_space=pltpu.VMEM)
    smem = pl.BlockSpec(memory_space=pltpu.SMEM)
    specs = [smem if arg.dtype == jnp.int32 else vmem for arg in args]
    placed = [
        arg if arg.dtype == jnp.int32 else pltpu.with_memory_space_constraint(arg, pltpu.VMEM)
        for arg in args
    ]
    specs += [pl.BlockSpec(memory_space=pltpu.HBM)] * len(raw)
    placed += [pltpu.with_memory_space_constraint(arg, pltpu.HBM) for arg in raw]
    return pl.pallas_call(
        kernel,
        out_shape=tuple(pltpu.VMEM(shape, dtype) for shape, dtype in outs),
        in_specs=specs,
        out_specs=(vmem,) * len(outs),
        compiler_params=pltpu.CompilerParams(vmem_limit_bytes=16 << 20),
        scratch_shapes=scratch,
    )(*placed)


def per_device(
    query_feats, key_feats, value_feats, out_gate, mr_filter, lr_rates, lr_residues, w_out
):
    channels, tokens = key_feats.shape
    group_count, modes = lr_rates.shape
    ctx_count = lax.axis_size(ctx_axes)
    z_count = lax.axis_size("zh")
    near_count = lax.axis_size(("x", "co"))
    mode_cols = group_count * modes
    kv_prod = (key_feats.astype(f32) * value_feats.astype(f32)).astype(bf16)
    rim = lax.ppermute(kv_prod, ctx_axes, [(i, i + 1) for i in range(ctx_count - 1)])
    place = jnp.stack([lax.axis_index(name) for name in ctx_axes]).astype(jnp.int32)
    mr_table, lr_table, collect, spread, decays, held_gate, query = on_chip(
        tables_kernel,
        (
            ((group_count, 2 * tokens, tokens), bf16),
            ((group_count, tokens, 2 * tokens), bf16),
            ((2, mode_cols, tokens), bf16),
            ((2, tokens, mode_cols), bf16),
            ((z_count, near_count, modes, channels), f32),
            ((tokens, channels), f32),
            ((channels, tokens), f32),
        ),
        place,
        mr_filter,
        lr_rates,
        lr_residues,
        out_gate,
        query_feats,
    )
    states, gated_mid = on_chip(
        blocks_kernel,
        (((near_count, modes, channels), f32), ((channels, tokens), bf16)),
        query,
        kv_prod,
        rim,
        mr_table,
        collect,
    )
    near_states = lax.all_to_all(
        states, ("x", "co"), split_axis=0, concat_axis=0, tiled=True
    )
    (local,) = on_chip(local_kernel, (((tokens, channels), f32),), gated_mid, lr_table)
    (row_states,) = on_chip(
        rows_kernel, (((z_count, modes, channels), f32),), near_states, decays
    )
    far_states = lax.all_to_all(row_states, "zh", split_axis=0, concat_axis=0, tiled=True)
    y_count, mid_count, low_count = (lax.axis_size(name) for name in tp_axes)
    width = w_out.shape[1] // (y_count * mid_count * low_count)
    (partial,) = on_chip(
        project_kernel,
        (((y_count, low_count, mid_count, tokens, width), bf16),),
        held_gate,
        local,
        far_states,
        spread,
        raw=(w_out,),
        scratch=(pltpu.VMEM(w_out.shape, bf16), pltpu.SemaphoreType.DMA((y_count,))),
    )
    near = lax.all_to_all(
        partial.reshape(y_count * low_count, mid_count, tokens, width),
        ("y", "zb"),
        split_axis=0,
        concat_axis=0,
        tiled=True,
    )
    near_sum = jnp.sum(near.astype(f32), axis=0).astype(bf16)
    far = lax.all_to_all(near_sum, "zq", split_axis=0, concat_axis=0, tiled=True)
    return jnp.sum(far.astype(f32), axis=0).T.astype(bf16)


def solution(mesh):
    ctx_count, tp_count = mesh.devices.shape
    finer = Mesh(
        mesh.devices.reshape(ctx_count // 8, 4, 2, tp_count // 8, 4, 2), ctx_axes + tp_axes
    )
    tiled = P(tp_axes, ctx_axes)
    rows = P(tp_axes, None)
    return jax.shard_map(
        per_device,
        mesh=finer,
        in_specs=(tiled, tiled, tiled, tiled, rows, rows, rows, rows),
        out_specs=tiled,
        check_vma=False,
    )
```

```python
import jax
import jax.numpy as jnp
from jax import lax
from jax.experimental import pallas as pl
from jax.experimental.pallas import tpu as pltpu
from jax.sharding import Mesh
from jax.sharding import PartitionSpec as P


chan_group = 16
ctx_axes = ("x", "zh", "co")
tp_axes = ("y", "zq", "zb")
f32 = jnp.float32
bf16 = jnp.bfloat16


def split_hi_lo(value):
    hi = value.astype(bf16)
    lo = (value - hi.astype(f32)).astype(bf16)
    return hi, lo


def dot(lhs, rhs, left=1, right=0, precision=None):
    return lax.dot_general(
        lhs,
        rhs,
        (((left,), (right,)), ((), ())),
        precision=precision,
        preferred_element_type=f32,
    )


def circulant(row, size):
    return pltpu.roll(jnp.broadcast_to(row, (size, size)), 0, 1, stride=1, stride_axis=0)


def same_block(row_count, col_count, row_width, col_width):
    rows = lax.broadcasted_iota(jnp.int32, (row_count, col_count), 0) // row_width
    cols = lax.broadcasted_iota(jnp.int32, (row_count, col_count), 1) // col_width
    return rows == cols


def laid_out(table):
    rows, cols = table.shape
    tiled = jnp.concatenate([table] * rows, axis=1)
    kept = jnp.where(same_block(rows, rows * cols, 1, cols), tiled, 0.0)
    return jnp.sum(kept, axis=0, keepdims=True)


def tables_kernel(
    place_ref,
    taps_ref,
    rates_ref,
    residues_ref,
    gate_ref,
    query_ref,
    mr_ref,
    lr_ref,
    collect_ref,
    spread_ref,
    decay_ref,
    held_gate_ref,
    held_query_ref,
):
    held_gate_ref[...] = gate_ref[...].astype(f32).T
    held_query_ref[...] = query_ref[...].astype(f32)
    group_count, block = taps_ref.shape
    modes = rates_ref.shape[1]
    mode_cols = group_count * modes
    z_count, near_count, _, channels = decay_ref.shape
    source = lax.broadcasted_iota(jnp.int32, (block, block), 0)
    target = lax.broadcasted_iota(jnp.int32, (block, block), 1)
    causal = target >= source

    rates = laid_out(rates_ref[...])
    weights = laid_out(residues_ref[...]) * jnp.sqrt(2.0 * rates / modes)
    steps = lax.broadcasted_iota(jnp.int32, (block, mode_cols), 0).astype(f32)
    spread = weights * jnp.exp(-rates * steps)
    spread_ref[0], spread_ref[1] = split_hi_lo(spread)
    collect = jnp.exp(-rates * (block - steps)).T
    collect_ref[0], collect_ref[1] = split_hi_lo(collect)
    pick = same_block(group_count, mode_cols, 1, modes).astype(f32)
    lr_taps = dot(pick, spread, 1, 1, lax.Precision.HIGHEST)
    mr_taps = taps_ref[...].astype(f32)
    for group in range(group_count):
        mr_circ = circulant(mr_taps[group : group + 1], block)
        mr_ref[group, :block] = jnp.where(causal, mr_circ, 0.0).astype(bf16)
        mr_ref[group, block:] = jnp.where(causal, 0.0, mr_circ).astype(bf16)
        lr_circ = jnp.where(causal, circulant(lr_taps[group : group + 1], block), 0.0)
        lr_hi, lr_lo = split_hi_lo(lr_circ)
        lr_ref[group, :, :block] = lr_hi
        lr_ref[group, :, block:] = lr_lo

    owner = same_block(group_count, channels, 1, chan_group).astype(f32)
    span = -block * dot(rates_ref[...], owner, 0, 0, lax.Precision.HIGHEST)
    x_here, z_here, core_here = place_ref[0], place_ref[1], place_ref[2]
    for z_to in range(z_count):
        into = (x_here * z_count + z_to) * 2 + core_here
        for near in range(near_count):
            out_of = (near // 2 * z_count + z_here) * 2 + near % 2
            gap = into - 1 - out_of
            decay = jnp.exp(span * jnp.maximum(gap, 0).astype(f32))
            decay_ref[z_to, near] = jnp.where(gap >= 0, decay, 0.0)


def blocks_kernel(query_ref, kv_ref, rim_ref, mr_ref, collect_ref, state_ref, gated_ref):
    channels, _ = kv_ref.shape
    group_count = mr_ref.shape[0]
    near_count, modes, _ = state_ref.shape
    both = jnp.concatenate([kv_ref[...], rim_ref[...]], axis=1)
    query = query_ref[...]
    gated_parts = []
    for group in range(group_count):
        rows = slice(group * chan_group, (group + 1) * chan_group)
        medium = dot(both[rows], mr_ref[group])
        gated_parts.append((query[rows] * medium).astype(bf16))
    gated = jnp.concatenate(gated_parts, axis=0)
    gated_ref[...] = gated
    mixed = dot(collect_ref[0], gated, 1, 1) + dot(collect_ref[1], gated, 1, 1)
    mixed = jnp.where(same_block(group_count * modes, channels, modes, chan_group), mixed, 0.0)
    state = jnp.sum(mixed.reshape(group_count, modes, channels), axis=0)
    for near in range(near_count):
        state_ref[near] = state


def local_filter(gated_ref, lr_ref):
    group_count, block, _ = lr_ref.shape
    parts = []
    for group in range(group_count):
        rows = slice(group * chan_group, (group + 1) * chan_group)
        wide = dot(gated_ref[rows], lr_ref[group])
        parts.append(wide[:, :block] + wide[:, block:])
    return jnp.concatenate(parts, axis=0).T


def rows_kernel(near_ref, decay_ref, out_ref):
    for z_to in range(out_ref.shape[0]):
        total = decay_ref[z_to, 0] * near_ref[0]
        for near in range(1, near_ref.shape[0]):
            total = total + decay_ref[z_to, near] * near_ref[near]
        out_ref[z_to] = total


def project_kernel(
    gate_ref, gated_ref, lr_ref, far_ref, spread_ref, w_hbm, out_ref, w_ref, sems
):
    y_count, low_count, mid_count, _, width = out_ref.shape
    span = low_count * mid_count * width
    copies = []
    for y_to in range(y_count):
        cols = slice(y_to * span, (y_to + 1) * span)
        copies.append(
            pltpu.make_async_copy(w_hbm.at[:, cols], w_ref.at[:, cols], sems.at[y_to])
        )
        copies[-1].start()
    far_count, modes, channels = far_ref.shape
    state = far_ref[0]
    for far in range(1, far_count):
        state = state + far_ref[far]
    mode_rows = spread_ref.shape[2]
    wide = jnp.concatenate([state] * (mode_rows // modes), axis=0)
    wide = jnp.where(same_block(mode_rows, channels, modes, chan_group), wide, 0.0)
    wide_hi, wide_lo = split_hi_lo(wide)
    carried = dot(spread_ref[0], wide_hi) + dot(spread_ref[0], wide_lo)
    carried = carried + dot(spread_ref[1], wide_hi)
    long_out = (local_filter(gated_ref, lr_ref) + carried).astype(bf16)
    held = (gate_ref[...] * long_out.astype(f32)).astype(bf16)
    for y_to in range(y_count):
        copies[y_to].wait()
        for mid in range(mid_count):
            for low in range(low_count):
                first = ((y_to * mid_count + mid) * low_count + low) * width
                total = dot(held, w_ref[:, first : first + width])
                out_ref[y_to, low, mid] = total.astype(bf16)


def on_chip(kernel, outs, *args, raw=(), scratch=()):
    vmem = pl.BlockSpec(memory_space=pltpu.VMEM)
    smem = pl.BlockSpec(memory_space=pltpu.SMEM)
    specs = [smem if arg.dtype == jnp.int32 else vmem for arg in args]
    placed = [
        arg if arg.dtype == jnp.int32 else pltpu.with_memory_space_constraint(arg, pltpu.VMEM)
        for arg in args
    ]
    specs += [pl.BlockSpec(memory_space=pltpu.HBM)] * len(raw)
    placed += [pltpu.with_memory_space_constraint(arg, pltpu.HBM) for arg in raw]
    return pl.pallas_call(
        kernel,
        out_shape=tuple(pltpu.VMEM(shape, dtype) for shape, dtype in outs),
        in_specs=specs,
        out_specs=(vmem,) * len(outs),
        compiler_params=pltpu.CompilerParams(vmem_limit_bytes=16 << 20),
        scratch_shapes=scratch,
    )(*placed)


def per_device(
    query_feats, key_feats, value_feats, out_gate, mr_filter, lr_rates, lr_residues, w_out
):
    channels, tokens = key_feats.shape
    group_count, modes = lr_rates.shape
    ctx_count = lax.axis_size(ctx_axes)
    z_count = lax.axis_size("zh")
    near_count = lax.axis_size(("x", "co"))
    mode_cols = group_count * modes
    kv_prod = (key_feats.astype(f32) * value_feats.astype(f32)).astype(bf16)
    rim = lax.ppermute(kv_prod, ctx_axes, [(i, i + 1) for i in range(ctx_count - 1)])
    place = jnp.stack([lax.axis_index(name) for name in ctx_axes]).astype(jnp.int32)
    mr_table, lr_table, collect, spread, decays, held_gate, query = on_chip(
        tables_kernel,
        (
            ((group_count, 2 * tokens, tokens), bf16),
            ((group_count, tokens, 2 * tokens), bf16),
            ((2, mode_cols, tokens), bf16),
            ((2, tokens, mode_cols), bf16),
            ((z_count, near_count, modes, channels), f32),
            ((tokens, channels), f32),
            ((channels, tokens), f32),
        ),
        place,
        mr_filter,
        lr_rates,
        lr_residues,
        out_gate,
        query_feats,
    )
    states, gated_mid = on_chip(
        blocks_kernel,
        (((near_count, modes, channels), f32), ((channels, tokens), bf16)),
        query,
        kv_prod,
        rim,
        mr_table,
        collect,
    )
    near_states = lax.all_to_all(
        states, ("x", "co"), split_axis=0, concat_axis=0, tiled=True
    )
    (row_states,) = on_chip(
        rows_kernel, (((z_count, modes, channels), f32),), near_states, decays
    )
    far_states = lax.all_to_all(row_states, "zh", split_axis=0, concat_axis=0, tiled=True)
    y_count, mid_count, low_count = (lax.axis_size(name) for name in tp_axes)
    width = w_out.shape[1] // (y_count * mid_count * low_count)
    (partial,) = on_chip(
        project_kernel,
        (((y_count, low_count, mid_count, tokens, width), bf16),),
        held_gate,
        gated_mid,
        lr_table,
        far_states,
        spread,
        raw=(w_out,),
        scratch=(pltpu.VMEM(w_out.shape, bf16), pltpu.SemaphoreType.DMA((y_count,))),
    )
    near = lax.all_to_all(
        partial.reshape(y_count * low_count, mid_count, tokens, width),
        ("y", "zb"),
        split_axis=0,
        concat_axis=0,
        tiled=True,
    )
    near_sum = jnp.sum(near.astype(f32), axis=0).astype(bf16)
    far = lax.all_to_all(near_sum, "zq", split_axis=0, concat_axis=0, tiled=True)
    return jnp.sum(far.astype(f32), axis=0).T.astype(bf16)


def solution(mesh):
    ctx_count, tp_count = mesh.devices.shape
    finer = Mesh(
        mesh.devices.reshape(ctx_count // 8, 4, 2, tp_count // 8, 4, 2), ctx_axes + tp_axes
    )
    tiled = P(tp_axes, ctx_axes)
    rows = P(tp_axes, None)
    return jax.shard_map(
        per_device,
        mesh=finer,
        in_specs=(tiled, tiled, tiled, tiled, rows, rows, rows, rows),
        out_specs=tiled,
        check_vma=False,
    )
```

```python
import jax
import jax.numpy as jnp
from jax import lax
from jax.experimental import pallas as pl
from jax.experimental.pallas import tpu as pltpu
from jax.sharding import Mesh
from jax.sharding import PartitionSpec as P


chan_group = 16
ctx_axes = ("x", "zh", "co")
tp_axes = ("y", "zq", "zb")
f32 = jnp.float32
bf16 = jnp.bfloat16


def split_hi_lo(value):
    hi = value.astype(bf16)
    lo = (value - hi.astype(f32)).astype(bf16)
    return hi, lo


def dot(lhs, rhs, left=1, right=0, precision=None):
    return lax.dot_general(
        lhs,
        rhs,
        (((left,), (right,)), ((), ())),
        precision=precision,
        preferred_element_type=f32,
    )


def circulant(row, size):
    return pltpu.roll(jnp.broadcast_to(row, (size, size)), 0, 1, stride=1, stride_axis=0)


def same_block(row_count, col_count, row_width, col_width):
    rows = lax.broadcasted_iota(jnp.int32, (row_count, col_count), 0) // row_width
    cols = lax.broadcasted_iota(jnp.int32, (row_count, col_count), 1) // col_width
    return rows == cols


def laid_out(table):
    rows, cols = table.shape
    tiled = jnp.concatenate([table] * rows, axis=1)
    kept = jnp.where(same_block(rows, rows * cols, 1, cols), tiled, 0.0)
    return jnp.sum(kept, axis=0, keepdims=True)


def tables_kernel(
    place_ref,
    taps_ref,
    rates_ref,
    residues_ref,
    gate_ref,
    query_ref,
    mr_ref,
    lr_ref,
    collect_ref,
    spread_ref,
    decay_ref,
    held_gate_ref,
    held_query_ref,
):
    held_gate_ref[...] = gate_ref[...].astype(f32).T
    held_query_ref[...] = query_ref[...].astype(f32)
    group_count, block = taps_ref.shape
    modes = rates_ref.shape[1]
    mode_cols = group_count * modes
    z_count, near_count, _, channels = decay_ref.shape
    source = lax.broadcasted_iota(jnp.int32, (block, block), 0)
    target = lax.broadcasted_iota(jnp.int32, (block, block), 1)
    causal = target >= source

    rates = laid_out(rates_ref[...])
    weights = laid_out(residues_ref[...]) * jnp.sqrt(2.0 * rates / modes)
    steps = lax.broadcasted_iota(jnp.int32, (block, mode_cols), 0).astype(f32)
    spread = weights * jnp.exp(-rates * steps)
    spread_ref[0], spread_ref[1] = split_hi_lo(spread)
    collect = jnp.exp(-rates * (block - steps)).T
    collect_ref[0], collect_ref[1] = split_hi_lo(collect)
    pick = same_block(group_count, mode_cols, 1, modes).astype(f32)
    lr_taps = dot(pick, spread, 1, 1, lax.Precision.HIGHEST)
    mr_taps = taps_ref[...].astype(f32)
    for group in range(group_count):
        mr_circ = circulant(mr_taps[group : group + 1], block)
        mr_ref[group, :block] = jnp.where(causal, mr_circ, 0.0).astype(bf16)
        mr_ref[group, block:] = jnp.where(causal, 0.0, mr_circ).astype(bf16)
        lr_circ = jnp.where(causal, circulant(lr_taps[group : group + 1], block), 0.0)
        lr_hi, lr_lo = split_hi_lo(lr_circ)
        lr_ref[group, :, :block] = lr_hi
        lr_ref[group, :, block:] = lr_lo

    owner = same_block(group_count, channels, 1, chan_group).astype(f32)
    span = -block * dot(rates_ref[...], owner, 0, 0, lax.Precision.HIGHEST)
    x_here, z_here, core_here = place_ref[0], place_ref[1], place_ref[2]
    for z_to in range(z_count):
        into = (x_here * z_count + z_to) * 2 + core_here
        for near in range(near_count):
            out_of = (near // 2 * z_count + z_here) * 2 + near % 2
            gap = into - 1 - out_of
            decay = jnp.exp(span * jnp.maximum(gap, 0).astype(f32))
            decay_ref[z_to, near] = jnp.where(gap >= 0, decay, 0.0)


def blocks_kernel(query_ref, kv_ref, rim_ref, mr_ref, collect_ref, state_ref, gated_ref):
    channels, _ = kv_ref.shape
    group_count = mr_ref.shape[0]
    near_count, modes, _ = state_ref.shape
    both = jnp.concatenate([kv_ref[...], rim_ref[...]], axis=1)
    query = query_ref[...]
    gated_parts = []
    for group in range(group_count):
        rows = slice(group * chan_group, (group + 1) * chan_group)
        medium = dot(both[rows], mr_ref[group])
        gated_parts.append((query[rows] * medium).astype(bf16))
    gated = jnp.concatenate(gated_parts, axis=0)
    gated_ref[...] = gated
    mixed = dot(collect_ref[0], gated, 1, 1) + dot(collect_ref[1], gated, 1, 1)
    mixed = jnp.where(same_block(group_count * modes, channels, modes, chan_group), mixed, 0.0)
    state = jnp.sum(mixed.reshape(group_count, modes, channels), axis=0)
    for near in range(near_count):
        state_ref[near] = state


def local_filter(gated_ref, lr_ref):
    group_count, block, _ = lr_ref.shape
    parts = []
    for group in range(group_count):
        rows = slice(group * chan_group, (group + 1) * chan_group)
        wide = dot(gated_ref[rows], lr_ref[group])
        parts.append(wide[:, :block] + wide[:, block:])
    return jnp.concatenate(parts, axis=0).T


def rows_kernel(near_ref, decay_ref, out_ref):
    for z_to in range(out_ref.shape[0]):
        total = decay_ref[z_to, 0] * near_ref[0]
        for near in range(1, near_ref.shape[0]):
            total = total + decay_ref[z_to, near] * near_ref[near]
        out_ref[z_to] = total


def project_kernel(
    gate_ref, gated_ref, lr_ref, far_ref, spread_ref, w_hbm, out_ref, w_ref, sems
):
    low_count, y_count, mid_count, _, width = out_ref.shape
    span = low_count * mid_count * width
    copies = []
    for y_to in range(y_count):
        cols = slice(y_to * span, (y_to + 1) * span)
        copies.append(
            pltpu.make_async_copy(w_hbm.at[:, cols], w_ref.at[:, cols], sems.at[y_to])
        )
        copies[-1].start()
    far_count, modes, channels = far_ref.shape
    state = far_ref[0]
    for far in range(1, far_count):
        state = state + far_ref[far]
    mode_rows = spread_ref.shape[2]
    wide = jnp.concatenate([state] * (mode_rows // modes), axis=0)
    wide = jnp.where(same_block(mode_rows, channels, modes, chan_group), wide, 0.0)
    wide_hi, wide_lo = split_hi_lo(wide)
    carried = dot(spread_ref[0], wide_hi) + dot(spread_ref[0], wide_lo)
    carried = carried + dot(spread_ref[1], wide_hi)
    long_out = (local_filter(gated_ref, lr_ref) + carried).astype(bf16)
    held = (gate_ref[...] * long_out.astype(f32)).astype(bf16)
    for y_to in range(y_count):
        copies[y_to].wait()
        for mid in range(mid_count):
            for low in range(low_count):
                first = ((y_to * mid_count + mid) * low_count + low) * width
                total = dot(held, w_ref[:, first : first + width])
                out_ref[low, y_to, mid] = total.astype(bf16)


def mixed_kernel(far_ref, out_ref):
    total = far_ref[0].astype(f32)
    for far in range(1, far_ref.shape[0]):
        total = total + far_ref[far].astype(f32)
    out_ref[...] = total.T.astype(bf16)


def on_chip(kernel, outs, *args, raw=(), scratch=()):
    vmem = pl.BlockSpec(memory_space=pltpu.VMEM)
    smem = pl.BlockSpec(memory_space=pltpu.SMEM)
    specs = [smem if arg.dtype == jnp.int32 else vmem for arg in args]
    placed = [
        arg if arg.dtype == jnp.int32 else pltpu.with_memory_space_constraint(arg, pltpu.VMEM)
        for arg in args
    ]
    specs += [pl.BlockSpec(memory_space=pltpu.HBM)] * len(raw)
    placed += [pltpu.with_memory_space_constraint(arg, pltpu.HBM) for arg in raw]
    return pl.pallas_call(
        kernel,
        out_shape=tuple(pltpu.VMEM(shape, dtype) for shape, dtype in outs),
        in_specs=specs,
        out_specs=(vmem,) * len(outs),
        compiler_params=pltpu.CompilerParams(vmem_limit_bytes=16 << 20),
        scratch_shapes=scratch,
    )(*placed)


def per_device(
    query_feats, key_feats, value_feats, out_gate, mr_filter, lr_rates, lr_residues, w_out
):
    channels, tokens = key_feats.shape
    group_count, modes = lr_rates.shape
    ctx_count = lax.axis_size(ctx_axes)
    z_count = lax.axis_size("zh")
    near_count = lax.axis_size(("x", "co"))
    mode_cols = group_count * modes
    kv_prod = (key_feats.astype(f32) * value_feats.astype(f32)).astype(bf16)
    rim = lax.ppermute(kv_prod, ctx_axes, [(i, i + 1) for i in range(ctx_count - 1)])
    place = jnp.stack([lax.axis_index(name) for name in ctx_axes]).astype(jnp.int32)
    mr_table, lr_table, collect, spread, decays, held_gate, query = on_chip(
        tables_kernel,
        (
            ((group_count, 2 * tokens, tokens), bf16),
            ((group_count, tokens, 2 * tokens), bf16),
            ((2, mode_cols, tokens), bf16),
            ((2, tokens, mode_cols), bf16),
            ((z_count, near_count, modes, channels), f32),
            ((tokens, channels), f32),
            ((channels, tokens), f32),
        ),
        place,
        mr_filter,
        lr_rates,
        lr_residues,
        out_gate,
        query_feats,
    )
    states, gated_mid = on_chip(
        blocks_kernel,
        (((near_count, modes, channels), f32), ((channels, tokens), bf16)),
        query,
        kv_prod,
        rim,
        mr_table,
        collect,
    )
    near_states = lax.all_to_all(
        states, ("x", "co"), split_axis=0, concat_axis=0, tiled=True
    )
    (row_states,) = on_chip(
        rows_kernel, (((z_count, modes, channels), f32),), near_states, decays
    )
    far_states = lax.all_to_all(row_states, "zh", split_axis=0, concat_axis=0, tiled=True)
    y_count, mid_count, low_count = (lax.axis_size(name) for name in tp_axes)
    width = w_out.shape[1] // (y_count * mid_count * low_count)
    (partial,) = on_chip(
        project_kernel,
        (((low_count, y_count, mid_count, tokens, width), bf16),),
        held_gate,
        gated_mid,
        lr_table,
        far_states,
        spread,
        raw=(w_out,),
        scratch=(pltpu.VMEM(w_out.shape, bf16), pltpu.SemaphoreType.DMA((y_count,))),
    )
    near = lax.all_to_all(
        partial.reshape(y_count * low_count, mid_count, tokens, width),
        ("zb", "y"),
        split_axis=0,
        concat_axis=0,
        tiled=True,
    )
    near_sum = jnp.sum(near.astype(f32), axis=0).astype(bf16)
    far = lax.all_to_all(near_sum, "zq", split_axis=0, concat_axis=0, tiled=True)
    return pl.pallas_call(
        mixed_kernel,
        out_shape=jax.ShapeDtypeStruct((width, tokens), bf16),
        in_specs=[pl.BlockSpec(memory_space=pltpu.VMEM)],
        out_specs=pl.BlockSpec(memory_space=pltpu.VMEM),
        compiler_params=pltpu.CompilerParams(vmem_limit_bytes=16 << 20),
    )(pltpu.with_memory_space_constraint(far, pltpu.VMEM))


def solution(mesh):
    ctx_count, tp_count = mesh.devices.shape
    finer = Mesh(
        mesh.devices.reshape(ctx_count // 8, 4, 2, tp_count // 8, 4, 2), ctx_axes + tp_axes
    )
    tiled = P(tp_axes, ctx_axes)
    rows = P(tp_axes, None)
    return jax.shard_map(
        per_device,
        mesh=finer,
        in_specs=(tiled, tiled, tiled, tiled, rows, rows, rows, rows),
        out_specs=tiled,
        check_vma=False,
    )
```
